32 devices in a mesh: groups: 2 (over y), vis: 8 (over z, x), band: 2 (over core).
Axes of the slice: x: 2, y: 2, z: 4, core: 2. Of those that a mesh axis runs over, the one named last changes fastest.
Arguments:
- pieces: bfloat16 [2, 3072, 128, 128], P('band', ('groups', 'vis')), parts along dimension 1, may hold values from -6 to 6
- visit: int32 [2, 3072], P('band', ('groups', 'vis')), parts along dimension 1, may hold values from 0 to 23
- tile_map: int32 [2, 3072, 1], P('band', ('groups', 'vis')), parts along dimension 1, may hold values from 0 to 7; in each aligned block of 192 rows (0 to 191, 192 to 383, ..., all dimensions but the last counted through in order) at most 48 rows name the same one
- good_columns: int32 [2, 3072, 4], P('band', ('groups', 'vis')), parts along dimension 1, may hold values from -2147483648 to 2147483646, as said below
- psf_taps: float32 [2, 3072, 2, 21], P('band', ('groups', 'vis')), parts along dimension 1, may hold values from 0.05 to 1
- shifts: float32 [2, 3072, 2], P('band', ('groups', 'vis')), parts along dimension 1, may hold values from -0.5 to 0.5
- calib: float32 [2, 24], P('band'), may hold values from 0.5 to 2
- weights: int32 [2, 24], P('band'), may hold values from 1 to 8
- band_gain: float32 [2], P('band'), may hold values from 0.5 to 2
Outputs:
- coadd: float32 [2, 2048, 128], P('band', ('groups', 'vis')), parts along dimension 1
- detection: float32 [2048, 128], P(('groups', 'vis')), parts along dimension 0
The draws below stay inside these ranges and needn't reach their ends.
There are 2 independent parts, one for each index of `groups`. The reference program is written for one: setup_inputs(seed, part) draws one part's arguments, and reference() takes and returns one part's arrays. A program takes and returns all parts, laid end to end along the dimension named above; an argument that names none is the same for every part. Nothing has to cross between parts.
Inputs may be any that keep to these rules, and one draw needn't show every extreme that they name: `tile_map`: among the 192 pieces of one band on one index of vis (aligned blocks of 192 pieces), no tile appears more than 48 times, a bound that some block reaches. `good_columns`: independent random bits.
All inputs are finite; a program needn't handle non-finite values.
Results may differ from the reference program's by a relative error of at most 0.0081.
Values may be sent and summed in bfloat16 or wider, within the bound.
No kernel may reach another device: no remote copies, remote signals or barrier semaphores. Data moves between devices by JAX's collectives and lax.ppermute only.
A program may use at most 128 MiB of HBM per device.

```python
import math
import jax
import jax.numpy as jnp
import numpy as np
from jax import lax

PIX = 128
PD = 192
VISITS = 24
KT = 21
BANDS = 2
TILES = 8
PIECES = 1536
WORDS = 4
CAP = 48
N_VIS = 8


def draw_good_columns(key, part):
    return jax.random.randint(key, (BANDS, PIECES, WORDS), -2147483648, 2147483647, dtype=jnp.int32)


def set_ends(values, key, least, top_value):
    longest = values.shape.index(max(values.shape))
    spots = []
    for shift in (0, 1):
        where = [jax.random.randint(jax.random.fold_in(key, axis), (), 0, length) for axis, length in enumerate(values.shape)]
        where[longest] = (where[longest] + shift) % values.shape[longest]
        spots.append(tuple(where))
    return values.at[spots[0]].set(least).at[spots[1]].set(top_value)


def block_levels(rng, dims, cuts, least, largest):
    level, own = 1.0, jax.random.fold_in(rng, 6)
    for dim, blocks in cuts:
        draws = jnp.exp(jax.random.uniform(jax.random.fold_in(own, dim), (blocks,), jnp.float32, least / len(cuts), largest / len(cuts)))
        level = level * jnp.repeat(draws, dims[dim] // blocks).reshape([-1 if axis == dim else 1 for axis in range(len(dims))])
    return level


def assign_block(own_key, own, number, rows, amount, top, bound, lean):
    ranking = jax.random.permutation(own_key, amount)
    crowded, usual = portions_of(amount, rows * top, bound, lean, True), portions_of(amount, rows * top, bound, lean, False)
    places = jnp.arange(amount)

    def named(sizes, rotation):
        used = int((sizes > 0).sum())
        fixed = max(1, used // 4)
        passed = fixed + (places - fixed + rotation * (used - fixed)) % max(1, amount - fixed)
        return jnp.zeros((amount,), jnp.int32).at[ranking[jnp.where(places < fixed, places, passed)]].set(jnp.asarray(sizes, jnp.int32))

    sizes = jnp.where(number % 4 == 0, named(crowded, number // 4), named(usual, number - number // 4 - 1))
    mixed = jax.random.permutation(jax.random.fold_in(own, 3), amount)
    donor, sink = mixed[0:amount // 2 * 2:2], mixed[1:amount // 2 * 2:2]
    room = jnp.minimum(sizes[donor] - 1, bound - sizes[sink]) // 2
    room = jnp.where((donor == ranking[0]) | (sink == ranking[0]) | (sizes[sink] == 0), 0, jnp.maximum(room, 0))
    passed = jax.random.randint(jax.random.fold_in(own, 4), (amount // 2,), 0, 1 << 20) % (room + 1)
    sizes = sizes.at[donor].add(-passed).at[sink].add(passed)
    members = jnp.searchsorted(jnp.cumsum(sizes), jnp.arange(rows * top), side="right").astype(jnp.int32)
    table = members.reshape(top, rows).T
    table = table[jax.random.permutation(jax.random.fold_in(own, 1), rows)]
    rotation = jax.random.randint(jax.random.fold_in(own, 2), (rows, 1), 0, top)
    return jnp.take_along_axis(table, (jnp.arange(top)[None, :] + rotation) % top, axis=1)


def portions_of(amount, total, most, skew, full):
    weights = [(1 << 20) // math.isqrt(rank ** skew) + 1 for rank in range(1, amount + 1)]
    largest = most if full else min(most, max(-(-total // amount), total * weights[0] // sum(weights)))
    least = 1 if total - largest >= amount - 1 else 0
    holding, spare = [largest] + [least] * (amount - 1), total - largest - least * (amount - 1)
    while spare > 0:
        free = [i for i in range(1, amount) if holding[i] < largest] or [i for i in range(1, amount) if holding[i] < most]
        pool, budget = sum([weights[i] for i in free]), spare
        for i in free:
            addition = min(most - holding[i], max(1, budget * weights[i] // pool), spare)
            holding[i] = holding[i] + addition
            spare = spare - addition
    return np.array(holding)


def bell_draw(rng, dims, deviation, most, shards=(), held_as=jnp.bfloat16):
    level = block_levels(rng, dims, shards, -0.22, 0.18) if shards else 1.0
    values = jax.random.normal(rng, dims, jnp.float32) * deviation * level
    return jnp.minimum(jnp.maximum(values, -most), most).astype(held_as)


def setup_inputs(seed: int = 0, part: int = 0) -> dict:
    arg_keys = jax.random.split(jax.random.key(seed), 10)
    own_keys = jax.random.split(jax.random.fold_in(arg_keys[9], part), 10)
    pieces = bell_draw(own_keys[0], (BANDS, PIECES, PIX, PIX), 1.0, 6.0, ((0, 2), (1, 8)))
    visit = set_ends(jax.random.randint(own_keys[1], (BANDS, PIECES), 0, VISITS), jax.random.fold_in(own_keys[1], 1), 0, VISITS - 1).astype(jnp.int32)
    tile_map_keys = jax.random.split(jax.random.fold_in(own_keys[2], 1), BANDS * PIECES // PD)
    tile_map_turns = jax.random.permutation(jax.random.fold_in(own_keys[2], 3), BANDS * PIECES // PD)
    tile_map = jax.vmap(lambda own, number: assign_block(jax.random.fold_in(own_keys[2], 2), own, number, PD, TILES, 1, CAP, 2))(tile_map_keys, tile_map_turns).reshape((BANDS, PIECES, 1))
    good_columns = draw_good_columns(jax.random.fold_in(jax.random.fold_in(arg_keys[9], part), 71), part)
    psf_taps = jnp.clip(jnp.exp(math.log(1.0) - 2.9957323 * jax.random.uniform(own_keys[4], (BANDS, PIECES, 2, KT), jnp.float32) ** block_levels(own_keys[4], (BANDS, PIECES, 2, KT), ((0, 2), (1, 8)), -0.2, 0.2)), 0.05, 1.0)
    shifts = jnp.clip(jax.random.uniform(own_keys[5], (BANDS, PIECES, 2), jnp.float32, -0.5, 0.5) * block_levels(own_keys[5], (BANDS, PIECES, 2), ((0, 2), (1, 8)), -0.4, 0.0), -0.5, 0.5)
    calib = jnp.clip(jnp.exp(math.log(2.0) - 1.3862944 * jax.random.uniform(arg_keys[6], (BANDS, VISITS), jnp.float32) ** block_levels(arg_keys[6], (BANDS, VISITS), ((0, 2),), -0.2, 0.2)), 0.5, 2.0)
    weights = set_ends(jax.random.randint(arg_keys[7], (BANDS, VISITS), 1, 9), jax.random.fold_in(arg_keys[7], 1), 1, 8).astype(jnp.int32)
    band_gain = jnp.clip(jnp.exp(math.log(2.0) - 1.3862944 * jax.random.uniform(arg_keys[8], (BANDS,), jnp.float32) ** block_levels(arg_keys[8], (BANDS,), ((0, 2),), -0.2, 0.2)), 0.5, 2.0)
    return {"pieces": pieces, "visit": visit, "tile_map": tile_map, "good_columns": good_columns, "psf_taps": psf_taps, "shifts": shifts, "calib": calib, "weights": weights, "band_gain": band_gain}


def good_mask(words):
    bits = jnp.arange(32, dtype=jnp.int32)
    flags = jnp.right_shift(words[..., None], bits) & 1
    return flags.reshape(words.shape[:-1] + (words.shape[-1] * 32,)).astype(jnp.float32)


def kernel_matrix(taps, size):
    kernel = taps / jnp.sum(taps, axis=-1, keepdims=True)
    reach = (taps.shape[-1] - 1) // 2
    result = jnp.zeros((taps.shape[0], size, size), jnp.float32)
    for tap in range(taps.shape[-1]):
        result = result + kernel[:, tap, None, None] * jnp.eye(size, k=tap - reach, dtype=jnp.float32)
    return result.astype(jnp.bfloat16)


def lanczos(values):
    inside = jnp.abs(values) < 3.0
    return jnp.where(inside, jnp.sinc(values) * jnp.sinc(values / 3.0), 0.0)


def warp_matrix(offset, size):
    places = jnp.arange(size).astype(jnp.float32)
    spread = places[None, None, :] - places[None, :, None] - offset[:, None, None]
    steps = jnp.arange(-3, 4).astype(jnp.float32)
    norms = jnp.sum(lanczos(steps[None, :] - offset[:, None]), axis=1)
    return (lanczos(spread) / norms[:, None, None]).astype(jnp.bfloat16)


def warp_pieces(pieces, visit, words, taps, shifts, calib, weights):
    size = pieces.shape[-1]
    good = good_mask(words)
    match = (visit[:, None] == jnp.arange(calib.shape[0], dtype=jnp.int32)[None, :]).astype(jnp.float32)
    scale = jnp.dot(match, calib, precision=lax.Precision.HIGHEST)
    weight = jnp.sum(match * weights.astype(jnp.float32)[None, :], axis=1)
    calibrated = (pieces.astype(jnp.float32) * scale[:, None, None] * good[:, None, :]).astype(jnp.bfloat16)
    w_rows = warp_matrix(shifts[:, 0], size).astype(jnp.float32)
    w_cols = warp_matrix(shifts[:, 1], size).astype(jnp.float32)
    k_rows = kernel_matrix(taps[:, 0], size).astype(jnp.float32)
    k_cols = kernel_matrix(taps[:, 1], size).astype(jnp.float32)
    left = jnp.einsum('pij,pjk->pik', w_rows, k_rows).astype(jnp.bfloat16)
    right = jnp.einsum('pij,pjk->pik', w_cols, k_cols).astype(jnp.bfloat16)
    inner = jnp.einsum('pij,pkj->pik', calibrated.astype(jnp.float32), right.astype(jnp.float32)).astype(jnp.bfloat16)
    warped = jnp.einsum('pij,pjk->pik', left.astype(jnp.float32), inner.astype(jnp.float32))
    num_piece = (warped * weight[:, None, None]).astype(jnp.bfloat16)
    row_weight = (jnp.sum(left.astype(jnp.float32), axis=2) * weight[:, None]).astype(jnp.bfloat16)
    col_good = jnp.einsum('pij,pj->pi', right.astype(jnp.float32), good).astype(jnp.bfloat16)
    return num_piece, row_weight, col_good


def reference(pieces, visit, tile_map, good_columns, psf_taps, shifts, calib, weights, band_gain):
    coadds = []
    detection = jnp.zeros((TILES * PIX, PIX), jnp.float32)
    for band in range(BANDS):
        def block(items):
            return warp_pieces(items[0], items[1], items[2], items[3], items[4], calib[band], weights[band])

        blocks = (pieces[band].reshape(N_VIS, PD, PIX, PIX), visit[band].reshape(N_VIS, PD),
                  good_columns[band].reshape(N_VIS, PD, WORDS), psf_taps[band].reshape(N_VIS, PD, 2, KT),
                  shifts[band].reshape(N_VIS, PD, 2))
        num_piece, row_weight, col_good = lax.map(block, blocks)
        num_piece = num_piece.reshape(PIECES, PIX, PIX)
        row_weight = row_weight.reshape(PIECES, PIX).astype(jnp.float32)
        col_good = col_good.reshape(PIECES, PIX).astype(jnp.float32)
        tile = tile_map[band, :, 0]
        num = jax.ops.segment_sum(num_piece.astype(jnp.float32), tile, num_segments=TILES)
        onehot = (tile[:, None] == jnp.arange(TILES, dtype=jnp.int32)[None, :]).astype(jnp.float32)

        def tile_den(column):
            return jnp.dot((row_weight * column[:, None]).T, col_good, precision=lax.Precision.HIGHEST)

        den = lax.map(tile_den, onehot.T)
        coadd = (num / jnp.maximum(den, 1.0)).reshape(TILES * PIX, PIX)
        coadds.append(coadd)
        detection = detection + band_gain[band] * coadd
    return jnp.stack(coadds, axis=0), detection
```

```python
import functools

import jax
import jax.numpy as jnp
import numpy as np
from jax import lax
from jax.experimental import pallas as pl
from jax.experimental.pallas import tpu as pltpu
from jax.sharding import PartitionSpec as P

EDGE = 3
ROWS = 16
SLOT = 32
GROUP = 4


def sinc(values):
    zero = values == 0.0
    scaled = jnp.where(zero, 1.0, values) * np.float32(np.pi)
    return jnp.where(zero, 1.0, jnp.sin(scaled) / scaled)


def lanczos(values):
    inside = jnp.abs(values) < float(EDGE)
    return jnp.where(inside, sinc(values) * sinc(values / float(EDGE)), 0.0)


def tap_vectors(taps, shift, pad_ref):
    count, n = taps.shape
    kernel = (taps / jnp.sum(taps, axis=0, keepdims=True)).astype(jnp.bfloat16)
    steps = range(-EDGE, EDGE + 1)
    window = [lanczos(float(m) - shift) for m in steps]
    norm = functools.reduce(jnp.add, window)
    window = [(w / norm).astype(jnp.bfloat16).astype(jnp.float32) for w in window]
    pad_ref[...] = jnp.zeros_like(pad_ref)
    pad_ref[pl.ds(8, count), :] = kernel.astype(jnp.float32)
    terms = [window[m + EDGE] * pad_ref[pl.ds(8 - m - EDGE, SLOT), :] for m in steps]
    first = [functools.reduce(jnp.add, terms[EDGE:])]
    for m in range(EDGE - 1, -1, -1):
        first.append(first[-1] + terms[m])
    last = [functools.reduce(jnp.add, terms[: EDGE + 1])]
    for m in range(EDGE + 1, 2 * EDGE):
        last.append(last[-1] + terms[m])
    kinds = first + last[::-1]
    return jnp.concatenate(kinds, axis=0).astype(jnp.bfloat16)


def kind_of(place, size):
    low = jnp.minimum(place, EDGE)
    return jnp.where(place >= size - EDGE, place - (size - EDGE) + EDGE + 1, low)


def table_block(block, size, halo, side):
    if block == 0:
        low, high = 0, EDGE + 1
    elif block == 1:
        low, high = EDGE, EDGE + 1
    else:
        low, high = EDGE, 2 * EDGE + 1
    depth = (high - low) * SLOT
    start = {0: 0, 1: ROWS, 2: size - ROWS}[block]
    tap = lax.broadcasted_iota(jnp.int32, (depth, size), 0)
    lane = lax.broadcasted_iota(jnp.int32, (1, size), 1)
    chunks = []
    for r in range(ROWS):
        row = start + r
        if side == 0:
            d = lane - row + halo
            kind = min(row, EDGE) if row < size - EDGE else row - (size - EDGE) + EDGE + 1
            slot = (kind - low) * SLOT + d
        else:
            d = row - lane + halo
            slot = (kind_of(lane, size) - low) * SLOT + d
        slot = jnp.where((d >= 0) & (d <= 2 * halo), slot, -1)
        chunks.append((tap == slot).astype(jnp.float32).astype(jnp.bfloat16))
    return low * SLOT, high * SLOT, jnp.concatenate(chunks, axis=1)


def fill_base(vectors_t, base_ref, size, halo, side):
    n = vectors_t.shape[0]
    for block in range(3):
        low, high, table = table_block(block, size, halo, side)
        out = jnp.dot(vectors_t[:, low:high], table, preferred_element_type=jnp.float32)
        for r in range(ROWS):
            base_ref[pl.ds((block * ROWS + r) * n, n), :] = out[:, r * size : (r + 1) * size]


def build(base_ref, p, n, size):
    blocks = []
    for block in range(3):
        halves = [
            base_ref[pl.ds((block * ROWS + 8 * h) * n + p, 8, stride=n), :] for h in range(ROWS // 8)
        ]
        blocks.append(jnp.concatenate(halves, axis=0))
    inner = [
        pltpu.roll(blocks[1], ROWS * b, 1).astype(jnp.bfloat16) for b in range(size // ROWS - 2)
    ]
    return jnp.concatenate(
        [blocks[0].astype(jnp.bfloat16)] + inner + [blocks[2].astype(jnp.bfloat16)], axis=0
    )


def kernel(
    tiles,
    tile_s,
    visit_s,
    words_s,
    calib_s,
    weights_s,
    tile_v,
    visit_v,
    taps_v,
    shifts_v,
    pieces_h,
    out_v,
    pieces_v,
    left_base,
    right_base,
    pad_ref,
    acc,
    cover,
    sems,
):
    n, size, _ = pieces_h.shape
    count = taps_v.shape[0]
    halo = (count - 1) // 2 + EDGE
    chunks = sems.shape[0]
    share = n // chunks
    copies = [
        pltpu.make_async_copy(
            pieces_h.at[pl.ds(c * share, share)], pieces_v.at[pl.ds(c * share, share)], sems.at[c]
        )
        for c in range(chunks)
    ]
    for copy in copies:
        copy.start()
    acc[...] = jnp.zeros_like(acc)
    vectors = []
    for side, base_ref in ((0, left_base), (1, right_base)):
        vec = tap_vectors(taps_v[:, side, :], shifts_v[pl.ds(side, 1), :], pad_ref)
        vectors.append(vec)
        fill_base(vec.astype(jnp.float32).T.astype(jnp.bfloat16), base_ref, size, halo, side)
    lane = lax.broadcasted_iota(jnp.int32, (8, size), 1)
    bit = lane & 31
    for copy in copies:
        copy.wait()

    def step(g, carry):
        for k in range(GROUP):
            p = g * GROUP + k
            word = jnp.where(
                lane < 64,
                jnp.where(lane < 32, words_s[0, p], words_s[1, p]),
                jnp.where(lane < 96, words_s[2, p], words_s[3, p]),
            )
            mask = (jnp.right_shift(word, bit) & 1).astype(jnp.float32)
            mask = jnp.concatenate([mask, mask], axis=0).astype(jnp.bfloat16)
            piece = pieces_v[p]
            rows = [piece[16 * b : 16 * b + 16] * mask for b in range(size // 16)] + [mask]
            right = build(right_base, p, n, size)
            inner = jnp.dot(
                jnp.concatenate(rows, axis=0), right, preferred_element_type=jnp.float32
            )
            cover[pl.ds(p, 1), :] = inner[size : size + 1]
            v = visit_s[0, p]
            factor = calib_s[0, v] * weights_s[0, v].astype(jnp.float32)
            inner = (inner[:size] * factor).astype(jnp.bfloat16)
            left = build(left_base, p, n, size)
            acc[tile_s[0, p]] += jnp.dot(left, inner, preferred_element_type=jnp.float32)
        return carry

    lax.fori_loop(0, n // GROUP, step, 0)

    kinds = 2 * EDGE + 1
    place = lax.broadcasted_iota(jnp.int32, (SLOT, kinds * SLOT), 0)
    row = jnp.where(place <= halo, place, place - (2 * halo + 1) + size)
    column = lax.broadcasted_iota(jnp.int32, (SLOT, kinds * SLOT), 1)
    d = (column & (SLOT - 1)) + row - halo
    chosen = (column // SLOT == kind_of(row, size)) & (d >= 0) & (d < size) & (row < size)
    table = chosen.astype(jnp.float32).astype(jnp.bfloat16)
    weight = jnp.zeros((1, n), jnp.float32)
    for v in range(weights_s.shape[1]):
        weight = jnp.where(visit_v[...] == v, weights_s[0, v].astype(jnp.float32), weight)
    row_weight = jnp.dot(table, vectors[0], preferred_element_type=jnp.float32) * weight
    chosen_rows = [jnp.where(tile_v[...] == t, row_weight, 0.0) for t in range(tiles)]
    den = jnp.dot(
        jnp.concatenate(chosen_rows, axis=0).astype(jnp.bfloat16),
        cover[...].astype(jnp.bfloat16),
        preferred_element_type=jnp.float32,
    )
    for t in range(tiles):
        out_v[t, :size, :] = acc[t].astype(out_v.dtype)
        out_v[t, size:, :] = den[t * SLOT : (t + 1) * SLOT].astype(out_v.dtype)


def partial_sums(tiles, pieces, visit, tile, words, taps, shifts, calib, weights):
    n, size, _ = pieces.shape
    smem = pl.BlockSpec(memory_space=pltpu.SMEM)
    vmem = pl.BlockSpec(memory_space=pltpu.VMEM)
    return pl.pallas_call(
        functools.partial(kernel, tiles),
        out_shape=jax.ShapeDtypeStruct((tiles, size + SLOT, size), jnp.bfloat16),
        in_specs=[smem] * 5 + [vmem] * 4 + [pl.BlockSpec(memory_space=pl.ANY)],
        out_specs=vmem,
        scratch_shapes=[
            pltpu.VMEM((n, size, size), jnp.bfloat16),
            pltpu.VMEM((3 * ROWS * n, size), jnp.float32),
            pltpu.VMEM((3 * ROWS * n, size), jnp.float32),
            pltpu.VMEM((SLOT + 16, n), jnp.float32),
            pltpu.VMEM((tiles, size, size), jnp.float32),
            pltpu.VMEM((n, size), jnp.float32),
            pltpu.SemaphoreType.DMA((4,)),
        ],
        compiler_params=pltpu.CompilerParams(vmem_limit_bytes=56 * 1024 * 1024),
        name="partial_sums",
    )(tile, visit, words, calib, weights, tile, visit, taps, shifts, pieces)


def shards(pieces, visit, tile_map, good_columns, psf_taps, shifts, calib, weights, band_gain):
    size = pieces.shape[-1]
    tiles = lax.axis_size("vis")
    halo = (psf_taps.shape[-1] - 1) // 2 + EDGE
    sums = partial_sums(
        tiles,
        pieces[0],
        visit,
        tile_map[:, :, 0],
        good_columns[0].T,
        jnp.transpose(psf_taps[0], (2, 1, 0)),
        shifts[0].T,
        calib,
        weights,
    )
    got = lax.all_to_all(sums, "vis", split_axis=0, concat_axis=0, tiled=True)
    total = jnp.sum(got.astype(jnp.float32), axis=0)
    few = total[size:]
    den = jnp.concatenate(
        [
            few[:halo],
            jnp.broadcast_to(few[halo], (size - 2 * halo, size)),
            few[halo + 1 : 2 * halo + 1],
        ],
        axis=0,
    )
    coadd = total[:size] / jnp.maximum(den, 1.0)
    scaled = band_gain[0] * coadd
    detection = scaled
    bands = lax.axis_size("band")
    for k in range(1, bands):
        detection = detection + lax.ppermute(
            scaled, "band", [(b, (b + k) % bands) for b in range(bands)]
        )
    return (coadd[None], detection)


def solution(mesh):
    placed = (
        P("band", ("groups", "vis"), None, None),
        P("band", ("groups", "vis")),
        P("band", ("groups", "vis"), None),
        P("band", ("groups", "vis"), None),
        P("band", ("groups", "vis"), None, None),
        P("band", ("groups", "vis"), None),
        P("band", None),
        P("band", None),
        P("band"),
    )
    return jax.shard_map(
        shards,
        mesh=mesh,
        in_specs=placed,
        out_specs=(P("band", ("groups", "vis"), None), P(("groups", "vis"), None)),
        check_vma=False,
    )
```

```python
import functools

import jax
import jax.numpy as jnp
import numpy as np
from jax import lax
from jax.experimental import pallas as pl
from jax.experimental.pallas import tpu as pltpu
from jax.sharding import PartitionSpec as P

EDGE = 3
ROWS = 16
SLOT = 32
GROUP = 16
PAD = 4


def sinc(values):
    zero = values == 0.0
    scaled = jnp.where(zero, 1.0, values) * np.float32(np.pi)
    return jnp.where(zero, 1.0, jnp.sin(scaled) / scaled)


def lanczos(values):
    inside = jnp.abs(values) < float(EDGE)
    return jnp.where(inside, sinc(values) * sinc(values / float(EDGE)), 0.0)


def tap_vectors(taps, shift, pad_ref):
    count, n = taps.shape
    kernel = (taps / jnp.sum(taps, axis=0, keepdims=True)).astype(jnp.bfloat16)
    steps = range(-EDGE, EDGE + 1)
    window = [lanczos(float(m) - shift) for m in steps]
    norm = functools.reduce(jnp.add, window)
    window = [(w / norm).astype(jnp.bfloat16).astype(jnp.float32) for w in window]
    pad_ref[...] = jnp.zeros_like(pad_ref)
    pad_ref[pl.ds(8, count), :] = kernel.astype(jnp.float32)
    terms = [window[m + EDGE] * pad_ref[pl.ds(8 - m - EDGE, SLOT), :] for m in steps]
    first = [functools.reduce(jnp.add, terms[EDGE:])]
    for m in range(EDGE - 1, -1, -1):
        first.append(first[-1] + terms[m])
    last = [functools.reduce(jnp.add, terms[: EDGE + 1])]
    for m in range(EDGE + 1, 2 * EDGE):
        last.append(last[-1] + terms[m])
    kinds = first + last[::-1]
    return jnp.concatenate(kinds, axis=0).astype(jnp.bfloat16)


def kind_of(place, size):
    low = jnp.minimum(place, EDGE)
    return jnp.where(place >= size - EDGE, place - (size - EDGE) + EDGE + 1, low)


def table_block(block, size, halo, side):
    if block == 0:
        low, high = 0, EDGE + 1
    elif block == 1:
        low, high = EDGE, EDGE + 1
    else:
        low, high = EDGE, 2 * EDGE + 1
    depth = (high - low) * SLOT
    start = {0: 0, 1: ROWS, 2: size - ROWS}[block]
    tap = lax.broadcasted_iota(jnp.int32, (depth, size), 0)
    lane = lax.broadcasted_iota(jnp.int32, (1, size), 1)
    chunks = []
    for r in range(ROWS):
        row = start + r
        if side == 0:
            d = lane - row + halo
            kind = min(row, EDGE) if row < size - EDGE else row - (size - EDGE) + EDGE + 1
            slot = (kind - low) * SLOT + d
        else:
            d = row - lane + halo
            slot = (kind_of(lane, size) - low) * SLOT + d
        slot = jnp.where((d >= 0) & (d <= 2 * halo), slot, -1)
        chunks.append((tap == slot).astype(jnp.float32).astype(jnp.bfloat16))
    return low * SLOT, high * SLOT, jnp.concatenate(chunks, axis=1)


def fill_base(vectors_t, base_ref, size, halo, side):
    n = vectors_t.shape[0]
    stride = n + PAD
    for block in range(3):
        low, high, table = table_block(block, size, halo, side)
        out = jnp.dot(vectors_t[:, low:high], table, preferred_element_type=jnp.float32)
        for r in range(ROWS):
            base_ref[pl.ds((block * ROWS + r) * stride, n), :] = out[:, r * size : (r + 1) * size]


def build(base_ref, p, n, size):
    stride = n + PAD
    blocks = []
    for block in range(3):
        halves = [
            base_ref[pl.ds((block * ROWS + 8 * h) * stride + p, 8, stride=stride), :] for h in range(ROWS // 8)
        ]
        blocks.append(jnp.concatenate(halves, axis=0).astype(jnp.bfloat16))
    inner = [pltpu.roll(blocks[1], ROWS * b, 1) for b in range(size // ROWS - 2)]
    return jnp.concatenate([blocks[0]] + inner + [blocks[2]], axis=0)


def kernel(
    tiles,
    tile_s,
    visit_s,
    words_s,
    calib_s,
    weights_s,
    tile_v,
    visit_v,
    taps_v,
    shifts_v,
    pieces_h,
    out_v,
    pieces_v,
    left_base,
    right_base,
    pad_ref,
    acc,
    cover,
    held,
    sems,
):
    n, size, _ = pieces_h.shape
    count = taps_v.shape[0]
    halo = (count - 1) // 2 + EDGE
    chunks = sems.shape[0]
    share = n // chunks
    copies = [
        pltpu.make_async_copy(
            pieces_h.at[pl.ds(c * share, share)], pieces_v.at[pl.ds(c * share, share)], sems.at[c]
        )
        for c in range(chunks)
    ]
    for copy in copies:
        copy.start()
    acc[...] = jnp.zeros_like(acc)
    vectors = []
    for side, base_ref in ((0, left_base), (1, right_base)):
        vec = tap_vectors(taps_v[:, side, :], shifts_v[pl.ds(side, 1), :], pad_ref)
        vectors.append(vec)
        fill_base(vec.astype(jnp.float32).T.astype(jnp.bfloat16), base_ref, size, halo, side)
    lane = lax.broadcasted_iota(jnp.int32, (8, size), 1)
    bit = lane & 31
    for copy in copies:
        copy.wait()

    def masked(p):
        word = jnp.where(
            lane < 64,
            jnp.where(lane < 32, words_s[0, p], words_s[1, p]),
            jnp.where(lane < 96, words_s[2, p], words_s[3, p]),
        )
        mask = (jnp.right_shift(word, bit) & 1).astype(jnp.float32)
        mask = jnp.concatenate([mask, mask], axis=0).astype(jnp.bfloat16)
        piece = pieces_v[p]
        rows = [piece[16 * b : 16 * b + 16] * mask for b in range(size // 16)] + [mask, mask]
        return jnp.concatenate(rows, axis=0)

    def columns(g):
        places = [g * GROUP + k for k in range(GROUP)]
        dots = [
            jnp.dot(masked(p), build(right_base, p, n, size), preferred_element_type=jnp.float32)
            for p in places
        ]
        for k, p in enumerate(places):
            cover[pl.ds(p, 1), :] = dots[k][size : size + 1]
            v = visit_s[0, p]
            factor = calib_s[0, v] * weights_s[0, v].astype(jnp.float32)
            held[k] = (dots[k][:size] * factor).astype(jnp.bfloat16)

    def rows(g):
        places = [g * GROUP + k for k in range(GROUP)]
        dots = [
            jnp.dot(build(left_base, p, n, size), held[k], preferred_element_type=jnp.float32)
            for k, p in enumerate(places)
        ]
        for k, p in enumerate(places):
            acc[tile_s[0, p]] += dots[k]

    def step(g, carry):
        columns(g)
        rows(g)
        return carry

    lax.fori_loop(0, n // GROUP, step, 0)

    kinds = 2 * EDGE + 1
    place = lax.broadcasted_iota(jnp.int32, (SLOT, kinds * SLOT), 0)
    row = jnp.where(place <= halo, place, place - (2 * halo + 1) + size)
    column = lax.broadcasted_iota(jnp.int32, (SLOT, kinds * SLOT), 1)
    d = (column & (SLOT - 1)) + row - halo
    chosen = (column // SLOT == kind_of(row, size)) & (d >= 0) & (d < size) & (row < size)
    table = chosen.astype(jnp.float32).astype(jnp.bfloat16)
    weight = jnp.zeros((1, n), jnp.float32)
    for v in range(weights_s.shape[1]):
        weight = jnp.where(visit_v[...] == v, weights_s[0, v].astype(jnp.float32), weight)
    row_weight = jnp.dot(table, vectors[0], preferred_element_type=jnp.float32) * weight
    chosen_rows = [jnp.where(tile_v[...] == t, row_weight, 0.0) for t in range(tiles)]
    den = jnp.dot(
        jnp.concatenate(chosen_rows, axis=0).astype(jnp.bfloat16),
        cover[...].astype(jnp.bfloat16),
        preferred_element_type=jnp.float32,
    )
    for t in range(tiles):
        out_v[t, :size, :] = acc[t].astype(out_v.dtype)
        out_v[t, size:, :] = den[t * SLOT : (t + 1) * SLOT].astype(out_v.dtype)


def partial_sums(tiles, pieces, visit, tile, words, taps, shifts, calib, weights):
    n, size, _ = pieces.shape
    smem = pl.BlockSpec(memory_space=pltpu.SMEM)
    vmem = pl.BlockSpec(memory_space=pltpu.VMEM)
    return pl.pallas_call(
        functools.partial(kernel, tiles),
        out_shape=jax.ShapeDtypeStruct((tiles, size + SLOT, size), jnp.bfloat16),
        in_specs=[smem] * 5 + [vmem] * 4 + [pl.BlockSpec(memory_space=pl.ANY)],
        out_specs=vmem,
        scratch_shapes=[
            pltpu.VMEM((n, size, size), jnp.bfloat16),
            pltpu.VMEM((3 * ROWS * (n + PAD), size), jnp.float32),
            pltpu.VMEM((3 * ROWS * (n + PAD), size), jnp.float32),
            pltpu.VMEM((SLOT + 16, n), jnp.float32),
            pltpu.VMEM((tiles, size, size), jnp.float32),
            pltpu.VMEM((n, size), jnp.float32),
            pltpu.VMEM((GROUP, size, size), jnp.bfloat16),
            pltpu.SemaphoreType.DMA((4,)),
        ],
        compiler_params=pltpu.CompilerParams(vmem_limit_bytes=56 * 1024 * 1024),
        name="partial_sums",
    )(tile, visit, words, calib, weights, tile, visit, taps, shifts, pieces)


def shards(pieces, visit, tile_map, good_columns, psf_taps, shifts, calib, weights, band_gain):
    size = pieces.shape[-1]
    tiles = lax.axis_size("vis")
    halo = (psf_taps.shape[-1] - 1) // 2 + EDGE
    sums = partial_sums(
        tiles,
        pieces[0],
        visit,
        tile_map[:, :, 0],
        good_columns[0].T,
        jnp.transpose(psf_taps[0], (2, 1, 0)),
        shifts[0].T,
        calib,
        weights,
    )
    got = lax.all_to_all(sums, "vis", split_axis=0, concat_axis=0, tiled=True)
    total = jnp.sum(got.astype(jnp.float32), axis=0)
    few = total[size:]
    den = jnp.concatenate(
        [
            few[:halo],
            jnp.broadcast_to(few[halo], (size - 2 * halo, size)),
            few[halo + 1 : 2 * halo + 1],
        ],
        axis=0,
    )
    coadd = total[:size] / jnp.maximum(den, 1.0)
    scaled = band_gain[0] * coadd
    detection = scaled
    bands = lax.axis_size("band")
    for k in range(1, bands):
        detection = detection + lax.ppermute(
            scaled, "band", [(b, (b + k) % bands) for b in range(bands)]
        )
    return (coadd[None], detection)


def solution(mesh):
    placed = (
        P("band", ("groups", "vis"), None, None),
        P("band", ("groups", "vis")),
        P("band", ("groups", "vis"), None),
        P("band", ("groups", "vis"), None),
        P("band", ("groups", "vis"), None, None),
        P("band", ("groups", "vis"), None),
        P("band", None),
        P("band", None),
        P("band"),
    )
    return jax.shard_map(
        shards,
        mesh=mesh,
        in_specs=placed,
        out_specs=(P("band", ("groups", "vis"), None), P(("groups", "vis"), None)),
        check_vma=False,
    )
```

```python
import functools

import jax
import jax.numpy as jnp
import numpy as np
from jax import lax
from jax.experimental import pallas as pl
from jax.experimental.pallas import tpu as pltpu
from jax.sharding import PartitionSpec as P

EDGE = 3
ROWS = 16
SLOT = 32
GROUP = 48
PAD = 4


def sinc(values):
    zero = values == 0.0
    scaled = jnp.where(zero, 1.0, values) * np.float32(np.pi)
    return jnp.where(zero, 1.0, jnp.sin(scaled) / scaled)


def lanczos(values):
    inside = jnp.abs(values) < float(EDGE)
    return jnp.where(inside, sinc(values) * sinc(values / float(EDGE)), 0.0)


def tap_vectors(taps, shift, pad_ref):
    count, n = taps.shape
    kernel = (taps / jnp.sum(taps, axis=0, keepdims=True)).astype(jnp.bfloat16)
    steps = range(-EDGE, EDGE + 1)
    window = [lanczos(float(m) - shift) for m in steps]
    norm = functools.reduce(jnp.add, window)
    window = [(w / norm).astype(jnp.bfloat16).astype(jnp.float32) for w in window]
    pad_ref[...] = jnp.zeros_like(pad_ref)
    pad_ref[pl.ds(8, count), :] = kernel.astype(jnp.float32)
    terms = [window[m + EDGE] * pad_ref[pl.ds(8 - m - EDGE, SLOT), :] for m in steps]
    first = [functools.reduce(jnp.add, terms[EDGE:])]
    for m in range(EDGE - 1, -1, -1):
        first.append(first[-1] + terms[m])
    last = [functools.reduce(jnp.add, terms[: EDGE + 1])]
    for m in range(EDGE + 1, 2 * EDGE):
        last.append(last[-1] + terms[m])
    kinds = first + last[::-1]
    return jnp.concatenate(kinds, axis=0).astype(jnp.bfloat16)


def kind_of(place, size):
    low = jnp.minimum(place, EDGE)
    return jnp.where(place >= size - EDGE, place - (size - EDGE) + EDGE + 1, low)


def table_block(block, size, halo, side):
    if block == 0:
        low, high = 0, EDGE + 1
    elif block == 1:
        low, high = EDGE, EDGE + 1
    else:
        low, high = EDGE, 2 * EDGE + 1
    depth = (high - low) * SLOT
    start = {0: 0, 1: ROWS, 2: size - ROWS}[block]
    tap = lax.broadcasted_iota(jnp.int32, (depth, size), 0)
    lane = lax.broadcasted_iota(jnp.int32, (1, size), 1)
    chunks = []
    for r in range(ROWS):
        row = start + r
        if side == 0:
            d = lane - row + halo
            kind = min(row, EDGE) if row < size - EDGE else row - (size - EDGE) + EDGE + 1
            slot = (kind - low) * SLOT + d
        else:
            d = row - lane + halo
            slot = (kind_of(lane, size) - low) * SLOT + d
        slot = jnp.where((d >= 0) & (d <= 2 * halo), slot, -1)
        chunks.append((tap == slot).astype(jnp.float32).astype(jnp.bfloat16))
    return low * SLOT, high * SLOT, jnp.concatenate(chunks, axis=1)


def fill_base(vectors_t, base_ref, size, halo, side):
    n = vectors_t.shape[0]
    stride = n + PAD
    for block in range(3):
        low, high, table = table_block(block, size, halo, side)
        out = jnp.dot(vectors_t[:, low:high], table, preferred_element_type=jnp.float32)
        for r in range(ROWS):
            base_ref[pl.ds((block * ROWS + r) * stride, n), :] = out[:, r * size : (r + 1) * size]


def build(base_ref, p, n, size):
    stride = n + PAD
    blocks = []
    for block in range(3):
        halves = [
            base_ref[pl.ds((block * ROWS + 8 * h) * stride + p, 8, stride=stride), :] for h in range(ROWS // 8)
        ]
        blocks.append(jnp.concatenate(halves, axis=0).astype(jnp.bfloat16))
    inner = [pltpu.roll(blocks[1], ROWS * b, 1) for b in range(size // ROWS - 2)]
    return jnp.concatenate([blocks[0]] + inner + [blocks[2]], axis=0)


def kernel(
    tiles,
    tile_s,
    visit_s,
    words_s,
    calib_s,
    weights_s,
    tile_v,
    visit_v,
    taps_v,
    shifts_v,
    pieces_h,
    out_v,
    pieces_v,
    left_base,
    right_base,
    pad_ref,
    acc,
    cover,
    held,
    sems,
):
    n, size, _ = pieces_h.shape
    count = taps_v.shape[0]
    halo = (count - 1) // 2 + EDGE
    share = GROUP
    chunks = n // share
    copies = [
        pltpu.make_async_copy(
            pieces_h.at[pl.ds(c * share, share)], pieces_v.at[pl.ds(c * share, share)], sems.at[c]
        )
        for c in range(chunks)
    ]
    for copy in copies:
        copy.start()
    acc[...] = jnp.zeros_like(acc)
    vectors = []
    for side, base_ref in ((0, left_base), (1, right_base)):
        vec = tap_vectors(taps_v[:, side, :], shifts_v[pl.ds(side, 1), :], pad_ref)
        vectors.append(vec)
        fill_base(vec.astype(jnp.float32).T.astype(jnp.bfloat16), base_ref, size, halo, side)
    lane = lax.broadcasted_iota(jnp.int32, (8, size), 1)
    bit = lane & 31
    def masked(p):
        word = jnp.where(
            lane < 64,
            jnp.where(lane < 32, words_s[0, p], words_s[1, p]),
            jnp.where(lane < 96, words_s[2, p], words_s[3, p]),
        )
        mask = (jnp.right_shift(word, bit) & 1).astype(jnp.float32)
        mask = jnp.concatenate([mask, mask], axis=0).astype(jnp.bfloat16)
        piece = pieces_v[p]
        rows = [piece[16 * b : 16 * b + 16] * mask for b in range(size // 16)] + [mask, mask]
        return jnp.concatenate(rows, axis=0)

    def columns(g):
        places = [g * GROUP + k for k in range(GROUP)]
        dots = [
            jnp.dot(masked(p), build(right_base, p, n, size), preferred_element_type=jnp.float32)
            for p in places
        ]
        for k, p in enumerate(places):
            cover[pl.ds(p, 1), :] = dots[k][size : size + 1]
            v = visit_s[0, p]
            factor = calib_s[0, v] * weights_s[0, v].astype(jnp.float32)
            held[k] = (dots[k][:size] * factor).astype(jnp.bfloat16)

    def rows(g):
        places = [g * GROUP + k for k in range(GROUP)]
        dots = [
            jnp.dot(build(left_base, p, n, size), held[k], preferred_element_type=jnp.float32)
            for k, p in enumerate(places)
        ]
        for k, p in enumerate(places):
            acc[tile_s[0, p]] += dots[k]

    def step(g, carry):
        spot = pl.ds(g * share, share)
        pltpu.make_async_copy(pieces_h.at[spot], pieces_v.at[spot], sems.at[g]).wait()
        columns(g)
        rows(g)
        return carry

    lax.fori_loop(0, n // GROUP, step, 0)

    kinds = 2 * EDGE + 1
    place = lax.broadcasted_iota(jnp.int32, (SLOT, kinds * SLOT), 0)
    row = jnp.where(place <= halo, place, place - (2 * halo + 1) + size)
    column = lax.broadcasted_iota(jnp.int32, (SLOT, kinds * SLOT), 1)
    d = (column & (SLOT - 1)) + row - halo
    chosen = (column // SLOT == kind_of(row, size)) & (d >= 0) & (d < size) & (row < size)
    table = chosen.astype(jnp.float32).astype(jnp.bfloat16)
    weight = jnp.zeros((1, n), jnp.float32)
    for v in range(weights_s.shape[1]):
        weight = jnp.where(visit_v[...] == v, weights_s[0, v].astype(jnp.float32), weight)
    row_weight = jnp.dot(table, vectors[0], preferred_element_type=jnp.float32) * weight
    chosen_rows = [jnp.where(tile_v[...] == t, row_weight, 0.0) for t in range(tiles)]
    den = jnp.dot(
        jnp.concatenate(chosen_rows, axis=0).astype(jnp.bfloat16),
        cover[...].astype(jnp.bfloat16),
        preferred_element_type=jnp.float32,
    )
    for t in range(tiles):
        out_v[t, :size, :] = acc[t].astype(out_v.dtype)
        out_v[t, size:, :] = den[t * SLOT : (t + 1) * SLOT].astype(out_v.dtype)


def partial_sums(tiles, pieces, visit, tile, words, taps, shifts, calib, weights):
    n, size, _ = pieces.shape
    smem = pl.BlockSpec(memory_space=pltpu.SMEM)
    vmem = pl.BlockSpec(memory_space=pltpu.VMEM)
    return pl.pallas_call(
        functools.partial(kernel, tiles),
        out_shape=jax.ShapeDtypeStruct((tiles, size + SLOT, size), jnp.bfloat16),
        in_specs=[smem] * 5 + [vmem] * 4 + [pl.BlockSpec(memory_space=pl.ANY)],
        out_specs=vmem,
        scratch_shapes=[
            pltpu.VMEM((n, size, size), jnp.bfloat16),
            pltpu.VMEM((3 * ROWS * (n + PAD), size), jnp.float32),
            pltpu.VMEM((3 * ROWS * (n + PAD), size), jnp.float32),
            pltpu.VMEM((SLOT + 16, n), jnp.float32),
            pltpu.VMEM((tiles, size, size), jnp.float32),
            pltpu.VMEM((n, size), jnp.float32),
            pltpu.VMEM((GROUP, size, size), jnp.bfloat16),
            pltpu.SemaphoreType.DMA((n // GROUP,)),
        ],
        compiler_params=pltpu.CompilerParams(vmem_limit_bytes=56 * 1024 * 1024),
        name="partial_sums",
    )(tile, visit, words, calib, weights, tile, visit, taps, shifts, pieces)


def shards(pieces, visit, tile_map, good_columns, psf_taps, shifts, calib, weights, band_gain):
    size = pieces.shape[-1]
    tiles = lax.axis_size("vis")
    halo = (psf_taps.shape[-1] - 1) // 2 + EDGE
    sums = partial_sums(
        tiles,
        pieces[0],
        visit,
        tile_map[:, :, 0],
        good_columns[0].T,
        jnp.transpose(psf_taps[0], (2, 1, 0)),
        shifts[0].T,
        calib,
        weights,
    )
    got = lax.all_to_all(sums, "vis", split_axis=0, concat_axis=0, tiled=True)
    total = jnp.sum(got.astype(jnp.float32), axis=0)
    few = total[size:]
    den = jnp.concatenate(
        [
            few[:halo],
            jnp.broadcast_to(few[halo], (size - 2 * halo, size)),
            few[halo + 1 : 2 * halo + 1],
        ],
        axis=0,
    )
    coadd = total[:size] / jnp.maximum(den, 1.0)
    scaled = band_gain[0] * coadd
    detection = scaled
    bands = lax.axis_size("band")
    for k in range(1, bands):
        detection = detection + lax.ppermute(
            scaled, "band", [(b, (b + k) % bands) for b in range(bands)]
        )
    return (coadd[None], detection)


def solution(mesh):
    placed = (
        P("band", ("groups", "vis"), None, None),
        P("band", ("groups", "vis")),
        P("band", ("groups", "vis"), None),
        P("band", ("groups", "vis"), None),
        P("band", ("groups", "vis"), None, None),
        P("band", ("groups", "vis"), None),
        P("band", None),
        P("band", None),
        P("band"),
    )
    return jax.shard_map(
        shards,
        mesh=mesh,
        in_specs=placed,
        out_specs=(P("band", ("groups", "vis"), None), P(("groups", "vis"), None)),
        check_vma=False,
    )
```

```python
import functools

import jax
import jax.numpy as jnp
import numpy as np
from jax import lax
from jax.experimental import pallas as pl
from jax.experimental.pallas import tpu as pltpu
from jax.sharding import PartitionSpec as P


EDGE = 3
ROWS = 16
SQUARE = 4
SLOT = 32
GROUP = 48
PAD = 4


def sinc(values):
    zero = values == 0.0
    scaled = jnp.where(zero, 1.0, values) * np.float32(np.pi)
    return jnp.where(zero, 1.0, jnp.sin(scaled) / scaled)


def lanczos(values):
    inside = jnp.abs(values) < float(EDGE)
    return jnp.where(inside, sinc(values) * sinc(values / float(EDGE)), 0.0)


def tap_vectors(taps, shift, pad_ref):
    count, _ = taps.shape
    kernel = (taps / jnp.sum(taps, axis=0, keepdims=True)).astype(jnp.bfloat16)
    steps = range(-EDGE, EDGE + 1)
    window = [lanczos(float(m) - shift) for m in steps]
    norm = functools.reduce(jnp.add, window)
    window = [(w / norm).astype(jnp.bfloat16).astype(jnp.float32) for w in window]
    pad_ref[...] = jnp.zeros_like(pad_ref)
    pad_ref[pl.ds(8, count), :] = kernel.astype(jnp.float32)
    terms = [window[m + EDGE] * pad_ref[pl.ds(8 - m - EDGE, SLOT), :] for m in steps]
    first = [functools.reduce(jnp.add, terms[EDGE:])]
    for m in range(EDGE - 1, -1, -1):
        first.append(first[-1] + terms[m])
    last = [functools.reduce(jnp.add, terms[: EDGE + 1])]
    for m in range(EDGE + 1, 2 * EDGE):
        last.append(last[-1] + terms[m])
    kinds = first + last[::-1]
    return jnp.concatenate(kinds, axis=0).astype(jnp.bfloat16)


def kind_of(place, size):
    low = jnp.minimum(place, EDGE)
    return jnp.where(place >= size - EDGE, place - (size - EDGE) + EDGE + 1, low)


def table_block(block, size, halo, side):
    if block == 0:
        low, high = 0, EDGE + 1
    elif block == 1:
        low, high = EDGE, EDGE + 1
    else:
        low, high = EDGE, 2 * EDGE + 1
    depth = (high - low) * SLOT
    start = {0: 0, 1: ROWS, 2: size - ROWS}[block]
    tap = lax.broadcasted_iota(jnp.int32, (depth, size), 0)
    lane = lax.broadcasted_iota(jnp.int32, (1, size), 1)
    chunks = []
    for r in range(ROWS):
        row = start + r
        if side == 0:
            d = lane - row + halo
            kind = min(row, EDGE) if row < size - EDGE else row - (size - EDGE) + EDGE + 1
            slot = (kind - low) * SLOT + d
        else:
            d = row - lane + halo
            slot = (kind_of(lane, size) - low) * SLOT + d
        slot = jnp.where((d >= 0) & (d <= 2 * halo), slot, -1)
        chunks.append((tap == slot).astype(jnp.float32).astype(jnp.bfloat16))
    return low * SLOT, high * SLOT, jnp.concatenate(chunks, axis=1)


def fill_base(vectors_t, base_ref, size, halo, side):
    n = vectors_t.shape[0]
    stride = n + PAD
    for block in range(3):
        low, high, table = table_block(block, size, halo, side)
        out = jnp.dot(vectors_t[:, low:high], table, preferred_element_type=jnp.float32)
        for r in range(ROWS):
            base_ref[pl.ds((block * ROWS + r) * stride, n), :] = out[:, r * size : (r + 1) * size]


def build(base_ref, p, n, size):
    stride = n + PAD
    blocks = []
    for block in range(3):
        halves = [
            base_ref[pl.ds((block * ROWS + 8 * h) * stride + p, 8, stride=stride), :] for h in range(ROWS // 8)
        ]
        blocks.append(jnp.concatenate(halves, axis=0).astype(jnp.bfloat16))
    inner = [pltpu.roll(blocks[1], ROWS * b, 1) for b in range(size // ROWS - 2)]
    return jnp.concatenate([blocks[0]] + inner + [blocks[2]], axis=0)


def kernel(
    tile_s,
    visit_s,
    words_s,
    calib_s,
    weights_s,
    tile_v,
    visit_v,
    taps_v,
    shifts_v,
    pieces_h,
    own_v,
    first_v,
    second_v,
    third_v,
    pieces_v,
    left_base,
    right_base,
    pad_ref,
    acc,
    cover,
    held,
    sems,
):
    outs = (own_v, first_v, second_v, third_v)
    rest = own_v.shape[0]
    me = lax.axis_index("vis")
    n, size, _ = pieces_h.shape
    count = taps_v.shape[0]
    halo = (count - 1) // 2 + EDGE
    share = GROUP
    chunks = n // share
    copies = [
        pltpu.make_async_copy(
            pieces_h.at[pl.ds(c * share, share)], pieces_v.at[pl.ds(c * share, share)], sems.at[c]
        )
        for c in range(chunks)
    ]
    for copy in copies:
        copy.start()
    acc[...] = jnp.zeros_like(acc)
    vectors = []
    for side, base_ref in ((0, left_base), (1, right_base)):
        vec = tap_vectors(taps_v[:, side, :], shifts_v[pl.ds(side, 1), :], pad_ref)
        vectors.append(vec)
        fill_base(vec.astype(jnp.float32).T.astype(jnp.bfloat16), base_ref, size, halo, side)
    lane = lax.broadcasted_iota(jnp.int32, (8, size), 1)
    bit = lane & 31

    def masked(p):
        word = jnp.where(
            lane < 64,
            jnp.where(lane < 32, words_s[0, p], words_s[1, p]),
            jnp.where(lane < 96, words_s[2, p], words_s[3, p]),
        )
        mask = (jnp.right_shift(word, bit) & 1).astype(jnp.float32)
        mask = jnp.concatenate([mask, mask], axis=0).astype(jnp.bfloat16)
        piece = pieces_v[p]
        rows = [piece[16 * b : 16 * b + 16] * mask for b in range(size // 16)] + [mask, mask]
        return jnp.concatenate(rows, axis=0)

    def columns(g):
        places = [g * GROUP + k for k in range(GROUP)]
        dots = [
            jnp.dot(masked(p), build(right_base, p, n, size), preferred_element_type=jnp.float32)
            for p in places
        ]
        for k, p in enumerate(places):
            cover[pl.ds(p, 1), :] = dots[k][size : size + 1]
            v = visit_s[0, p]
            factor = calib_s[0, v] * weights_s[0, v].astype(jnp.float32)
            held[k] = (dots[k][:size] * factor).astype(jnp.bfloat16)

    def rows(g):
        places = [g * GROUP + k for k in range(GROUP)]
        dots = [
            jnp.dot(build(left_base, p, n, size), held[k], preferred_element_type=jnp.float32)
            for k, p in enumerate(places)
        ]
        for k, p in enumerate(places):
            place = tile_s[0, p] ^ me
            acc[(place & (SQUARE - 1)) * rest + lax.div(place, SQUARE)] += dots[k]

    def step(g, carry):
        spot = pl.ds(g * share, share)
        pltpu.make_async_copy(pieces_h.at[spot], pieces_v.at[spot], sems.at[g]).wait()
        columns(g)
        rows(g)
        return carry

    lax.fori_loop(0, n // GROUP, step, 0)

    kinds = 2 * EDGE + 1
    place = lax.broadcasted_iota(jnp.int32, (SLOT, kinds * SLOT), 0)
    row = jnp.where(place <= halo, place, place - (2 * halo + 1) + size)
    column = lax.broadcasted_iota(jnp.int32, (SLOT, kinds * SLOT), 1)
    d = (column & (SLOT - 1)) + row - halo
    chosen = (column // SLOT == kind_of(row, size)) & (d >= 0) & (d < size) & (row < size)
    table = chosen.astype(jnp.float32).astype(jnp.bfloat16)
    weight = jnp.zeros((1, n), jnp.float32)
    for v in range(weights_s.shape[1]):
        weight = jnp.where(visit_v[...] == v, weights_s[0, v].astype(jnp.float32), weight)
    row_weight = jnp.dot(table, vectors[0], preferred_element_type=jnp.float32) * weight
    for k, out_v in enumerate(outs):
        chosen_rows = [
            jnp.where(tile_v[...] == (SQUARE * j + k) ^ me, row_weight, 0.0) for j in range(rest)
        ]
        den = jnp.dot(
            jnp.concatenate(chosen_rows, axis=0).astype(jnp.bfloat16),
            cover[...].astype(jnp.bfloat16),
            preferred_element_type=jnp.float32,
        )
        for j in range(rest):
            out_v[j, :size, :] = acc[k * rest + j].astype(out_v.dtype)
            out_v[j, size:, :] = den[j * SLOT : (j + 1) * SLOT].astype(out_v.dtype)


def partial_sums(tiles, pieces, visit, tile, words, taps, shifts, calib, weights):
    n, size, _ = pieces.shape
    smem = pl.BlockSpec(memory_space=pltpu.SMEM)
    vmem = pl.BlockSpec(memory_space=pltpu.VMEM)
    return pl.pallas_call(
        kernel,
        out_shape=[
            jax.ShapeDtypeStruct((tiles // SQUARE, size + SLOT, size), jnp.bfloat16 if k else jnp.float32)
            for k in range(SQUARE)
        ],
        in_specs=[smem] * 5 + [vmem] * 4 + [pl.BlockSpec(memory_space=pl.ANY)],
        out_specs=[vmem] * SQUARE,
        scratch_shapes=[
            pltpu.VMEM((n, size, size), jnp.bfloat16),
            pltpu.VMEM((3 * ROWS * (n + PAD), size), jnp.float32),
            pltpu.VMEM((3 * ROWS * (n + PAD), size), jnp.float32),
            pltpu.VMEM((SLOT + 16, n), jnp.float32),
            pltpu.VMEM((tiles, size, size), jnp.float32),
            pltpu.VMEM((n, size), jnp.float32),
            pltpu.VMEM((GROUP, size, size), jnp.bfloat16),
            pltpu.SemaphoreType.DMA((n // GROUP,)),
        ],
        compiler_params=pltpu.CompilerParams(vmem_limit_bytes=28 * 1024 * 1024),
        name="partial_sums",
    )(*(
        pltpu.with_memory_space_constraint(x, pltpu.HBM)
        for x in (tile, visit, words, calib, weights, tile, visit, taps, shifts, pieces)
    ))


def shards(pieces, visit, tile_map, good_columns, psf_taps, shifts, calib, weights, band_gain):
    size = pieces.shape[-1]
    tiles = lax.axis_size("vis")
    halo = (psf_taps.shape[-1] - 1) // 2 + EDGE
    sums = partial_sums(
        tiles,
        pieces[0],
        visit,
        tile_map[:, :, 0],
        good_columns[0].T,
        jnp.transpose(psf_taps[0], (2, 1, 0)),
        shifts[0].T,
        calib,
        weights,
    )
    own, *others = sums
    got = []
    for k in range(SQUARE - 1, 0, -1):
        got.append(lax.ppermute(others[k - 1], "vis", [(i, i ^ k) for i in range(tiles)]))
    joint = [
        own[j] + functools.reduce(jnp.add, [g[j].astype(jnp.float32) for g in got])
        for j in range(tiles // SQUARE)
    ]
    total = joint[0]
    for j in range(1, tiles // SQUARE):
        ring = [(i, i ^ (SQUARE * j)) for i in range(tiles)]
        total = total + lax.ppermute(joint[j].astype(jnp.bfloat16), "vis", ring).astype(jnp.float32)
    few = total[size:]
    den = jnp.concatenate(
        [
            few[:halo],
            jnp.broadcast_to(few[halo], (size - 2 * halo, size)),
            few[halo + 1 : 2 * halo + 1],
        ],
        axis=0,
    )
    coadd = total[:size] / jnp.maximum(den, 1.0)
    scaled = band_gain[0] * coadd
    detection = scaled
    bands = lax.axis_size("band")
    for k in range(1, bands):
        detection = detection + lax.ppermute(
            scaled, "band", [(b, (b + k) % bands) for b in range(bands)]
        )
    return (coadd[None], detection)


def solution(mesh):
    placed = (
        P("band", ("groups", "vis"), None, None),
        P("band", ("groups", "vis")),
        P("band", ("groups", "vis"), None),
        P("band", ("groups", "vis"), None),
        P("band", ("groups", "vis"), None, None),
        P("band", ("groups", "vis"), None),
        P("band", None),
        P("band", None),
        P("band"),
    )
    return jax.shard_map(
        shards,
        mesh=mesh,
        in_specs=placed,
        out_specs=(P("band", ("groups", "vis"), None), P(("groups", "vis"), None)),
        check_vma=False,
    )
```

```python
import functools

import jax
import jax.numpy as jnp
import numpy as np
from jax import lax
from jax.experimental import pallas as pl
from jax.experimental.pallas import tpu as pltpu
from jax.sharding import PartitionSpec as P


EDGE = 3
ROWS = 16
SQUARE = 4
SLOT = 32
GROUP = 96
PAD = 4


def sinc(values):
    zero = values == 0.0
    scaled = jnp.where(zero, 1.0, values) * np.float32(np.pi)
    return jnp.where(zero, 1.0, jnp.sin(scaled) / scaled)


def lanczos(values):
    inside = jnp.abs(values) < float(EDGE)
    return jnp.where(inside, sinc(values) * sinc(values / float(EDGE)), 0.0)


def tap_vectors(taps, shift, pad_ref):
    count, _ = taps.shape
    kernel = (taps / jnp.sum(taps, axis=0, keepdims=True)).astype(jnp.bfloat16)
    steps = range(-EDGE, EDGE + 1)
    window = [lanczos(float(m) - shift) for m in steps]
    norm = functools.reduce(jnp.add, window)
    window = [(w / norm).astype(jnp.bfloat16).astype(jnp.float32) for w in window]
    pad_ref[...] = jnp.zeros_like(pad_ref)
    pad_ref[pl.ds(8, count), :] = kernel.astype(jnp.float32)
    terms = [window[m + EDGE] * pad_ref[pl.ds(8 - m - EDGE, SLOT), :] for m in steps]
    first = [functools.reduce(jnp.add, terms[EDGE:])]
    for m in range(EDGE - 1, -1, -1):
        first.append(first[-1] + terms[m])
    last = [functools.reduce(jnp.add, terms[: EDGE + 1])]
    for m in range(EDGE + 1, 2 * EDGE):
        last.append(last[-1] + terms[m])
    kinds = first + last[::-1]
    return jnp.concatenate(kinds, axis=0).astype(jnp.bfloat16)


def kind_of(place, size):
    low = jnp.minimum(place, EDGE)
    return jnp.where(place >= size - EDGE, place - (size - EDGE) + EDGE + 1, low)


def table_block(block, size, halo, side):
    if block == 0:
        low, high = 0, EDGE + 1
    elif block == 1:
        low, high = EDGE, EDGE + 1
    else:
        low, high = EDGE, 2 * EDGE + 1
    depth = (high - low) * SLOT
    start = {0: 0, 1: ROWS, 2: size - ROWS}[block]
    tap = lax.broadcasted_iota(jnp.int32, (depth, size), 0)
    lane = lax.broadcasted_iota(jnp.int32, (1, size), 1)
    chunks = []
    for r in range(ROWS):
        row = start + r
        if side == 0:
            d = lane - row + halo
            kind = min(row, EDGE) if row < size - EDGE else row - (size - EDGE) + EDGE + 1
            slot = (kind - low) * SLOT + d
        else:
            d = row - lane + halo
            slot = (kind_of(lane, size) - low) * SLOT + d
        slot = jnp.where((d >= 0) & (d <= 2 * halo), slot, -1)
        chunks.append((tap == slot).astype(jnp.float32).astype(jnp.bfloat16))
    return low * SLOT, high * SLOT, jnp.concatenate(chunks, axis=1)


def fill_base(vectors_t, base_ref, size, halo, side):
    n = vectors_t.shape[0]
    stride = n + PAD
    for block in range(3):
        low, high, table = table_block(block, size, halo, side)
        out = jnp.dot(vectors_t[:, low:high], table, preferred_element_type=jnp.float32)
        for r in range(ROWS):
            base_ref[pl.ds((block * ROWS + r) * stride, n), :] = out[:, r * size : (r + 1) * size]


def build(base_ref, p, n, size):
    stride = n + PAD
    blocks = []
    for block in range(3):
        halves = [
            base_ref[pl.ds((block * ROWS + 8 * h) * stride + p, 8, stride=stride), :] for h in range(ROWS // 8)
        ]
        blocks.append(jnp.concatenate(halves, axis=0).astype(jnp.bfloat16))
    inner = [pltpu.roll(blocks[1], ROWS * b, 1) for b in range(size // ROWS - 2)]
    return jnp.concatenate([blocks[0]] + inner + [blocks[2]], axis=0)


def kernel(
    tile_s,
    visit_s,
    words_s,
    calib_s,
    weights_s,
    tile_v,
    visit_v,
    taps_v,
    shifts_v,
    pieces_h,
    own_v,
    first_v,
    second_v,
    third_v,
    pieces_v,
    left_base,
    right_base,
    pad_ref,
    acc,
    cover,
    held,
    sems,
):
    outs = (own_v, first_v, second_v, third_v)
    rest = own_v.shape[0]
    me = lax.axis_index("vis")
    n, size, _ = pieces_h.shape
    count = taps_v.shape[0]
    halo = (count - 1) // 2 + EDGE
    share = GROUP
    chunks = n // share
    copies = [
        pltpu.make_async_copy(
            pieces_h.at[pl.ds(c * share, share)], pieces_v.at[pl.ds(c * share, share)], sems.at[c]
        )
        for c in range(chunks)
    ]
    for copy in copies:
        copy.start()
    acc[...] = jnp.zeros_like(acc)
    vectors = []
    for side, base_ref in ((0, left_base), (1, right_base)):
        vec = tap_vectors(taps_v[:, side, :], shifts_v[pl.ds(side, 1), :], pad_ref)
        vectors.append(vec)
        fill_base(vec.astype(jnp.float32).T.astype(jnp.bfloat16), base_ref, size, halo, side)
    lane = lax.broadcasted_iota(jnp.int32, (8, size), 1)
    bit = lane & 31

    def masked(p):
        word = jnp.where(
            lane < 64,
            jnp.where(lane < 32, words_s[0, p], words_s[1, p]),
            jnp.where(lane < 96, words_s[2, p], words_s[3, p]),
        )
        mask = (jnp.right_shift(word, bit) & 1).astype(jnp.float32)
        mask = jnp.concatenate([mask, mask], axis=0).astype(jnp.bfloat16)
        piece = pieces_v[p]
        rows = [piece[16 * b : 16 * b + 16] * mask for b in range(size // 16)] + [mask, mask]
        return jnp.concatenate(rows, axis=0)

    def columns(g):
        places = [g * GROUP + k for k in range(GROUP)]
        dots = [
            jnp.dot(masked(p), build(right_base, p, n, size), preferred_element_type=jnp.float32)
            for p in places
        ]
        for k, p in enumerate(places):
            cover[pl.ds(p, 1), :] = dots[k][size : size + 1]
            v = visit_s[0, p]
            factor = calib_s[0, v] * weights_s[0, v].astype(jnp.float32)
            held[k] = (dots[k][:size] * factor).astype(jnp.bfloat16)

    def rows(g):
        places = [g * GROUP + k for k in range(GROUP)]
        dots = [
            jnp.dot(build(left_base, p, n, size), held[k], preferred_element_type=jnp.float32)
            for k, p in enumerate(places)
        ]
        for k, p in enumerate(places):
            place = tile_s[0, p] ^ me
            acc[(place & (SQUARE - 1)) * rest + lax.div(place, SQUARE)] += dots[k]

    def step(g, carry):
        spot = pl.ds(g * share, share)
        pltpu.make_async_copy(pieces_h.at[spot], pieces_v.at[spot], sems.at[g]).wait()
        columns(g)
        rows(g)
        return carry

    lax.fori_loop(0, n // GROUP, step, 0)

    kinds = 2 * EDGE + 1
    place = lax.broadcasted_iota(jnp.int32, (SLOT, kinds * SLOT), 0)
    row = jnp.where(place <= halo, place, place - (2 * halo + 1) + size)
    column = lax.broadcasted_iota(jnp.int32, (SLOT, kinds * SLOT), 1)
    d = (column & (SLOT - 1)) + row - halo
    chosen = (column // SLOT == kind_of(row, size)) & (d >= 0) & (d < size) & (row < size)
    table = chosen.astype(jnp.float32).astype(jnp.bfloat16)
    weight = jnp.zeros((1, n), jnp.float32)
    for v in range(weights_s.shape[1]):
        weight = jnp.where(visit_v[...] == v, weights_s[0, v].astype(jnp.float32), weight)
    row_weight = jnp.dot(table, vectors[0], preferred_element_type=jnp.float32) * weight
    for k, out_v in enumerate(outs):
        chosen_rows = [
            jnp.where(tile_v[...] == (SQUARE * j + k) ^ me, row_weight, 0.0) for j in range(rest)
        ]
        den = jnp.dot(
            jnp.concatenate(chosen_rows, axis=0).astype(jnp.bfloat16),
            cover[...].astype(jnp.bfloat16),
            preferred_element_type=jnp.float32,
        )
        for j in range(rest):
            out_v[j, :size, :] = acc[k * rest + j].astype(out_v.dtype)
            out_v[j, size:, :] = den[j * SLOT : (j + 1) * SLOT].astype(out_v.dtype)


def partial_sums(tiles, pieces, visit, tile, words, taps, shifts, calib, weights):
    n, size, _ = pieces.shape
    smem = pl.BlockSpec(memory_space=pltpu.SMEM)
    vmem = pl.BlockSpec(memory_space=pltpu.VMEM)
    return pl.pallas_call(
        kernel,
        out_shape=[
            jax.ShapeDtypeStruct((tiles // SQUARE, size + SLOT, size), jnp.bfloat16 if k else jnp.float32)
            for k in range(SQUARE)
        ],
        in_specs=[smem] * 5 + [vmem] * 4 + [pl.BlockSpec(memory_space=pl.ANY)],
        out_specs=[vmem] * SQUARE,
        scratch_shapes=[
            pltpu.VMEM((n, size, size), jnp.bfloat16),
            pltpu.VMEM((3 * ROWS * (n + PAD), size), jnp.float32),
            pltpu.VMEM((3 * ROWS * (n + PAD), size), jnp.float32),
            pltpu.VMEM((SLOT + 16, n), jnp.float32),
            pltpu.VMEM((tiles, size, size), jnp.float32),
            pltpu.VMEM((n, size), jnp.float32),
            pltpu.VMEM((GROUP, size, size), jnp.bfloat16),
            pltpu.SemaphoreType.DMA((n // GROUP,)),
        ],
        compiler_params=pltpu.CompilerParams(vmem_limit_bytes=28 * 1024 * 1024),
        name="partial_sums",
    )(*(
        pltpu.with_memory_space_constraint(x, pltpu.HBM)
        for x in (tile, visit, words, calib, weights, tile, visit, taps, shifts, pieces)
    ))


def shards(pieces, visit, tile_map, good_columns, psf_taps, shifts, calib, weights, band_gain):
    size = pieces.shape[-1]
    tiles = lax.axis_size("vis")
    halo = (psf_taps.shape[-1] - 1) // 2 + EDGE
    sums = partial_sums(
        tiles,
        pieces[0],
        visit,
        tile_map[:, :, 0],
        good_columns[0].T,
        jnp.transpose(psf_taps[0], (2, 1, 0)),
        shifts[0].T,
        calib,
        weights,
    )
    own, *others = sums
    got = []
    for k in range(SQUARE - 1, 0, -1):
        got.append(lax.ppermute(others[k - 1], "vis", [(i, i ^ k) for i in range(tiles)]))
    joint = [
        own[j] + functools.reduce(jnp.add, [g[j].astype(jnp.float32) for g in got])
        for j in range(tiles // SQUARE)
    ]
    total = joint[0]
    for j in range(1, tiles // SQUARE):
        ring = [(i, i ^ (SQUARE * j)) for i in range(tiles)]
        total = total + lax.ppermute(joint[j].astype(jnp.bfloat16), "vis", ring).astype(jnp.float32)

    def weighed(sums):
        few = sums[size:]
        den = jnp.concatenate(
            [
                few[:halo],
                jnp.broadcast_to(few[halo], (size - 2 * halo, size)),
                few[halo + 1 : 2 * halo + 1],
            ],
            axis=0,
        )
        return sums[:size] / jnp.maximum(den, 1.0)

    scaled = band_gain[0] * weighed(total)
    detection = scaled
    bands = lax.axis_size("band")
    for k in range(1, bands):
        detection = detection + lax.ppermute(
            scaled, "band", [(b, (b + k) % bands) for b in range(bands)]
        )
    coadd = weighed(lax.optimization_barrier(total))
    return (coadd[None], detection)


def solution(mesh):
    placed = (
        P("band", ("groups", "vis"), None, None),
        P("band", ("groups", "vis")),
        P("band", ("groups", "vis"), None),
        P("band", ("groups", "vis"), None),
        P("band", ("groups", "vis"), None, None),
        P("band", ("groups", "vis"), None),
        P("band", None),
        P("band", None),
        P("band"),
    )
    return jax.shard_map(
        shards,
        mesh=mesh,
        in_specs=placed,
        out_specs=(P("band", ("groups", "vis"), None), P(("groups", "vis"), None)),
        check_vma=False,
    )
```

```python
import functools

import jax
import jax.numpy as jnp
import numpy as np
from jax import lax
from jax.experimental import pallas as pl
from jax.experimental.pallas import tpu as pltpu
from jax.sharding import PartitionSpec as P


EDGE = 3
ROWS = 16
SQUARE = 4
SLOT = 32
GROUP = 96
PAD = 4


def sinc(values):
    zero = values == 0.0
    scaled = jnp.where(zero, 1.0, values) * np.float32(np.pi)
    return jnp.where(zero, 1.0, jnp.sin(scaled) / scaled)


def lanczos(values):
    inside = jnp.abs(values) < float(EDGE)
    return jnp.where(inside, sinc(values) * sinc(values / float(EDGE)), 0.0)


def tap_vectors(taps, shift, pad_ref):
    count, _ = taps.shape
    kernel = (taps / jnp.sum(taps, axis=0, keepdims=True)).astype(jnp.bfloat16)
    steps = range(-EDGE, EDGE + 1)
    window = [lanczos(float(m) - shift) for m in steps]
    norm = functools.reduce(jnp.add, window)
    window = [(w / norm).astype(jnp.bfloat16).astype(jnp.float32) for w in window]
    pad_ref[...] = jnp.zeros_like(pad_ref)
    pad_ref[pl.ds(8, count), :] = kernel.astype(jnp.float32)
    terms = [window[m + EDGE] * pad_ref[pl.ds(8 - m - EDGE, SLOT), :] for m in steps]
    first = [functools.reduce(jnp.add, terms[EDGE:])]
    for m in range(EDGE - 1, -1, -1):
        first.append(first[-1] + terms[m])
    last = [functools.reduce(jnp.add, terms[: EDGE + 1])]
    for m in range(EDGE + 1, 2 * EDGE):
        last.append(last[-1] + terms[m])
    kinds = first + last[::-1]
    return jnp.concatenate(kinds, axis=0).astype(jnp.bfloat16)


def kind_of(place, size):
    low = jnp.minimum(place, EDGE)
    return jnp.where(place >= size - EDGE, place - (size - EDGE) + EDGE + 1, low)


def table_block(block, size, halo, side):
    if block == 0:
        low, high = 0, EDGE + 1
    elif block == 1:
        low, high = EDGE, EDGE + 1
    else:
        low, high = EDGE, 2 * EDGE + 1
    depth = (high - low) * SLOT
    start = {0: 0, 1: ROWS, 2: size - ROWS}[block]
    tap = lax.broadcasted_iota(jnp.int32, (depth, size), 0)
    lane = lax.broadcasted_iota(jnp.int32, (1, size), 1)
    near = lax.broadcasted_iota(jnp.int32, (SLOT, size), 0)
    far = lax.broadcasted_iota(jnp.int32, (SLOT, size), 1)
    ahead = far - near if side == 0 else -far - near
    chunks = []
    for r in range(ROWS):
        row = start + r
        kind = min(row, EDGE) if row < size - EDGE else row - (size - EDGE) + EDGE + 1
        if side == 0 or block == 1:
            kind = kind if side == 0 else EDGE
            taps = (ahead == (row - halo if side == 0 else -row - halo)).astype(jnp.float32)
            parts = [jnp.zeros((rows, size), jnp.bfloat16) for rows in ((kind - low) * SLOT, (high - 1 - kind) * SLOT)]
            parts.insert(1, taps.astype(jnp.bfloat16))
            chunks.append(jnp.concatenate([x for x in parts if x.shape[0]], axis=0))
            continue
        d = row - lane + halo
        slot = (kind_of(lane, size) - low) * SLOT + d
        slot = jnp.where((d >= 0) & (d <= 2 * halo), slot, -1)
        chunks.append((tap == slot).astype(jnp.float32).astype(jnp.bfloat16))
    return low * SLOT, high * SLOT, jnp.concatenate(chunks, axis=1)


def fill_base(vectors_t, base_ref, size, halo, side):
    n = vectors_t.shape[0]
    stride = n + PAD
    for block in range(3):
        low, high, table = table_block(block, size, halo, side)
        out = jnp.dot(vectors_t[:, low:high], table, preferred_element_type=jnp.float32)
        for r in range(ROWS):
            base_ref[pl.ds((block * ROWS + r) * stride, n), :] = out[:, r * size : (r + 1) * size]


def build(base_ref, p, n, size):
    stride = n + PAD
    blocks = []
    for block in range(3):
        halves = [
            base_ref[pl.ds((block * ROWS + 8 * h) * stride + p, 8, stride=stride), :] for h in range(ROWS // 8)
        ]
        blocks.append(jnp.concatenate(halves, axis=0).astype(jnp.bfloat16))
    inner = [pltpu.roll(blocks[1], ROWS * b, 1) for b in range(size // ROWS - 2)]
    return jnp.concatenate([blocks[0]] + inner + [blocks[2]], axis=0)


def kernel(
    tile_s,
    visit_s,
    words_s,
    calib_s,
    weights_s,
    tile_v,
    visit_v,
    taps_v,
    shifts_v,
    pieces_h,
    own_v,
    first_v,
    second_v,
    third_v,
    pieces_v,
    left_base,
    right_base,
    pad_ref,
    acc,
    cover,
    held,
    sems,
):
    outs = (own_v, first_v, second_v, third_v)
    rest = own_v.shape[0]
    me = lax.axis_index("vis")
    n, size, _ = pieces_h.shape
    count = taps_v.shape[0]
    halo = (count - 1) // 2 + EDGE
    share = GROUP
    chunks = n // share
    copies = [
        pltpu.make_async_copy(
            pieces_h.at[pl.ds(c * share, share)], pieces_v.at[pl.ds(c * share, share)], sems.at[c]
        )
        for c in range(chunks)
    ]
    for copy in copies:
        copy.start()
    acc[...] = jnp.zeros_like(acc)
    vectors = []
    for side, base_ref in ((0, left_base), (1, right_base)):
        vec = tap_vectors(taps_v[:, side, :], shifts_v[pl.ds(side, 1), :], pad_ref)
        vectors.append(vec)
        fill_base(vec.astype(jnp.float32).T.astype(jnp.bfloat16), base_ref, size, halo, side)
    lane = lax.broadcasted_iota(jnp.int32, (8, size), 1)
    bit = lane & 31

    def masked(p):
        word = jnp.where(
            lane < 64,
            jnp.where(lane < 32, words_s[0, p], words_s[1, p]),
            jnp.where(lane < 96, words_s[2, p], words_s[3, p]),
        )
        mask = (jnp.right_shift(word, bit) & 1).astype(jnp.float32)
        mask = jnp.concatenate([mask, mask], axis=0).astype(jnp.bfloat16)
        piece = pieces_v[p]
        rows = [piece[16 * b : 16 * b + 16] * mask for b in range(size // 16)] + [mask, mask]
        return jnp.concatenate(rows, axis=0)

    def columns(g):
        places = [g * GROUP + k for k in range(GROUP)]
        dots = [
            jnp.dot(masked(p), build(right_base, p, n, size), preferred_element_type=jnp.float32)
            for p in places
        ]
        for k, p in enumerate(places):
            cover[pl.ds(p, 1), :] = dots[k][size : size + 1]
            v = visit_s[0, p]
            factor = calib_s[0, v] * weights_s[0, v].astype(jnp.float32)
            held[k] = (dots[k][:size] * factor).astype(jnp.bfloat16)

    def rows(g):
        places = [g * GROUP + k for k in range(GROUP)]
        dots = [
            jnp.dot(build(left_base, p, n, size), held[k], preferred_element_type=jnp.float32)
            for k, p in enumerate(places)
        ]
        for k, p in enumerate(places):
            place = tile_s[0, p] ^ me
            acc[(place & (SQUARE - 1)) * rest + lax.div(place, SQUARE)] += dots[k]

    def step(g, carry):
        spot = pl.ds(g * share, share)
        pltpu.make_async_copy(pieces_h.at[spot], pieces_v.at[spot], sems.at[g]).wait()
        columns(g)
        rows(g)
        return carry

    lax.fori_loop(0, n // GROUP, step, 0)

    kinds = 2 * EDGE + 1
    place = lax.broadcasted_iota(jnp.int32, (SLOT, kinds * SLOT), 0)
    row = jnp.where(place <= halo, place, place - (2 * halo + 1) + size)
    column = lax.broadcasted_iota(jnp.int32, (SLOT, kinds * SLOT), 1)
    d = (column & (SLOT - 1)) + row - halo
    chosen = (column // SLOT == kind_of(row, size)) & (d >= 0) & (d < size) & (row < size)
    table = chosen.astype(jnp.float32).astype(jnp.bfloat16)
    weight = jnp.zeros((1, n), jnp.float32)
    for v in range(weights_s.shape[1]):
        weight = jnp.where(visit_v[...] == v, weights_s[0, v].astype(jnp.float32), weight)
    row_weight = jnp.dot(table, vectors[0], preferred_element_type=jnp.float32) * weight
    for k, out_v in enumerate(outs):
        chosen_rows = [
            jnp.where(tile_v[...] == (SQUARE * j + k) ^ me, row_weight, 0.0) for j in range(rest)
        ]
        den = jnp.dot(
            jnp.concatenate(chosen_rows, axis=0).astype(jnp.bfloat16),
            cover[...].astype(jnp.bfloat16),
            preferred_element_type=jnp.float32,
        )
        for j in range(rest):
            out_v[j, :size, :] = acc[k * rest + j].astype(out_v.dtype)
            out_v[j, size:, :] = den[j * SLOT : (j + 1) * SLOT].astype(out_v.dtype)


def partial_sums(tiles, pieces, visit, tile, words, taps, shifts, calib, weights):
    n, size, _ = pieces.shape
    smem = pl.BlockSpec(memory_space=pltpu.SMEM)
    vmem = pl.BlockSpec(memory_space=pltpu.VMEM)
    return pl.pallas_call(
        kernel,
        out_shape=[
            jax.ShapeDtypeStruct((tiles // SQUARE, size + SLOT, size), jnp.bfloat16 if k else jnp.float32)
            for k in range(SQUARE)
        ],
        in_specs=[smem] * 5 + [vmem] * 4 + [pl.BlockSpec(memory_space=pl.ANY)],
        out_specs=[vmem] * SQUARE,
        scratch_shapes=[
            pltpu.VMEM((n, size, size), jnp.bfloat16),
            pltpu.VMEM((3 * ROWS * (n + PAD), size), jnp.float32),
            pltpu.VMEM((3 * ROWS * (n + PAD), size), jnp.float32),
            pltpu.VMEM((SLOT + 16, n), jnp.float32),
            pltpu.VMEM((tiles, size, size), jnp.float32),
            pltpu.VMEM((n, size), jnp.float32),
            pltpu.VMEM((GROUP, size, size), jnp.bfloat16),
            pltpu.SemaphoreType.DMA((n // GROUP,)),
        ],
        compiler_params=pltpu.CompilerParams(vmem_limit_bytes=28 * 1024 * 1024),
        name="partial_sums",
    )(*(
        pltpu.with_memory_space_constraint(x, pltpu.HBM)
        for x in (tile, visit, words, calib, weights, tile, visit, taps, shifts, pieces)
    ))


def shards(pieces, visit, tile_map, good_columns, psf_taps, shifts, calib, weights, band_gain):
    size = pieces.shape[-1]
    tiles = lax.axis_size("vis")
    halo = (psf_taps.shape[-1] - 1) // 2 + EDGE
    sums = partial_sums(
        tiles,
        pieces[0],
        visit,
        tile_map[:, :, 0],
        good_columns[0].T,
        jnp.transpose(psf_taps[0], (2, 1, 0)),
        shifts[0].T,
        calib,
        weights,
    )
    own, *others = sums
    got = []
    for k in range(SQUARE - 1, 0, -1):
        got.append(lax.ppermute(others[k - 1], "vis", [(i, i ^ k) for i in range(tiles)]))
    joint = [
        own[j] + functools.reduce(jnp.add, [g[j].astype(jnp.float32) for g in got])
        for j in range(tiles // SQUARE)
    ]
    total = joint[0]
    for j in range(1, tiles // SQUARE):
        ring = [(i, i ^ (SQUARE * j)) for i in range(tiles)]
        total = total + lax.ppermute(joint[j].astype(jnp.bfloat16), "vis", ring).astype(jnp.float32)

    def weighed(sums):
        few = sums[size:]
        den = jnp.concatenate(
            [
                few[:halo],
                jnp.broadcast_to(few[halo], (size - 2 * halo, size)),
                few[halo + 1 : 2 * halo + 1],
            ],
            axis=0,
        )
        return sums[:size] / jnp.maximum(den, 1.0)

    scaled = band_gain[0] * weighed(total)
    detection = scaled
    bands = lax.axis_size("band")
    for k in range(1, bands):
        detection = detection + lax.ppermute(
            scaled, "band", [(b, (b + k) % bands) for b in range(bands)]
        )
    coadd = weighed(lax.optimization_barrier(total))
    return (coadd[None], detection)


def solution(mesh):
    placed = (
        P("band", ("groups", "vis"), None, None),
        P("band", ("groups", "vis")),
        P("band", ("groups", "vis"), None),
        P("band", ("groups", "vis"), None),
        P("band", ("groups", "vis"), None, None),
        P("band", ("groups", "vis"), None),
        P("band", None),
        P("band", None),
        P("band"),
    )
    return jax.shard_map(
        shards,
        mesh=mesh,
        in_specs=placed,
        out_specs=(P("band", ("groups", "vis"), None), P(("groups", "vis"), None)),
        check_vma=False,
    )
```
